32 devices in a mesh: rad: 8 (over z, y), ell: 4 (over x, core).
Axes of the slice: x: 2, y: 2, z: 4, core: 2. Of those that a mesh axis runs over, the one named last changes fastest.
Arguments:
- field: bfloat16 [512, 128, 512], P('rad', 'ell'), may hold values from -6 to 6
- projection: bfloat16 [512, 128, 256], P('rad', 'ell'), may hold values from -0.375 to 0.375
- ell_ids: int32 [128], P('ell'), may hold values from 0 to 255, as said below
Outputs:
- share: float32 [128, 256], P('ell', 'rad')
- crest: float32 [128, 256], P('ell', 'rad')
The draws below stay inside these ranges and needn't reach their ends.
Inputs may be any that keep to these rules, and one draw needn't show every extreme that they name: `ell_ids`: distinct and ascending.
All inputs are finite; a program needn't handle non-finite values.
Results may differ from the reference program's by a relative error of at most 0.0003.
Values may be sent and summed in bfloat16 or wider, within the bound.
A program may use at most 64 MiB of HBM per device.

```python
import jax
import jax.numpy as jnp

LMAX = 256
M = 512
R = 512
N = 256
ELLS = 128


def draw_ell_ids(key, part):
    chosen = jax.random.permutation(jax.random.fold_in(key, 11), LMAX)[:ELLS]
    return jnp.sort(chosen).astype(jnp.int32)


def spiked(result, own_key, source, target, shards_of, factor):
    owner, partner = [(jnp.arange(result.shape[dim]) // (result.shape[dim] // shards_of)).reshape([-1 if axis == dim else 1 for axis in range(result.ndim)]) for dim in (source, target)]
    chosen = jax.random.permutation(own_key, shards_of)[partner]
    strong = (owner == chosen) | (owner == (partner + shards_of // 2) % shards_of)
    return jnp.where(strong, factor * result, result)


def level_of(rng, dims, pieces, least, largest):
    factor_of, own = 1.0, jax.random.fold_in(rng, 6)
    for axis_at, shards_of in pieces:
        draws = jnp.exp(jax.random.uniform(jax.random.fold_in(own, axis_at), (shards_of,), jnp.float32, least / len(pieces), largest / len(pieces)))
        factor_of = factor_of * jnp.repeat(draws, dims[axis_at] // shards_of).reshape([-1 if axis == axis_at else 1 for axis in range(len(dims))])
    return factor_of


def gaussian(own_key, shape, spread, reach, shards=(), kind=jnp.bfloat16):
    values = spread * jax.random.normal(own_key, shape, jnp.float32)
    if shards:
        values = values * level_of(own_key, shape, shards, -0.22, 0.18)
    return jnp.clip(values, -reach, reach).astype(kind)


def heavy_noise(own_key, extent, deviation, most, cuts, heavy, kind=jnp.bfloat16):
    result = deviation * jax.random.normal(own_key, extent, jnp.float32)
    if cuts:
        result = result * level_of(own_key, extent, cuts, -0.22, 0.18)
    return jnp.clip(spiked(result, jax.random.fold_in(own_key, 3), *heavy), -most, most).astype(kind)


def setup_inputs(seed: int = 0) -> dict:
    arg_keys = jax.random.split(jax.random.key(seed), 4)
    return {
        "field": gaussian(arg_keys[0], (R, ELLS, M), 1.0, 6.0, ((0, 8), (1, 4))),
        "projection": heavy_noise(arg_keys[1], (R, ELLS, N), R ** -0.5, 0.375, ((0, 8), (1, 4)), (0, 2, 8, 2.0)),
        "ell_ids": draw_ell_ids(jax.random.fold_in(arg_keys[3], 71), 0),
    }


def reference(field, projection, ell_ids):
    coef = jnp.einsum("rem,ren->emn", field.astype(jnp.float32), projection.astype(jnp.float32))
    slots = jnp.arange(M, dtype=jnp.int32)
    valid = (slots[None, :] < (2 * ell_ids[:, None] + 1)).astype(jnp.float32)
    energy = jnp.sum(valid[:, :, None] * coef * coef, axis=1)
    peak = jnp.max(valid[:, :, None] * jnp.abs(coef), axis=1)
    column = jnp.sum(energy, axis=0) + 1e-6
    top = jnp.max(peak, axis=0) + 1e-6
    share = ELLS * energy / column[None, :]
    crest = peak / top[None, :]
    return share, crest
```

```python
import functools

import jax
import jax.numpy as jnp
from jax import lax
from jax.experimental import pallas as pl
from jax.experimental.pallas import tpu as pltpu
from jax.sharding import PartitionSpec as P

MESH = pl.DeviceIdType.MESH


def flipped(me, step, n):
    peer, bit = 0, 1
    while bit < n:
        b = (me // bit) % 2
        peer = peer + bit * ((1 - b) if step & bit else b)
        bit *= 2
    return peer


def project_kernel(n, n_ell, own, depth, m_size, n_size, ell_ref, fp_ref, energy_ref, peak_ref, total_ref,
                   held, mine, stats, mine2, totals,
                   send_sem, recv_sem, local_sem, send2, recv2, send3, recv3):
    me = lax.axis_index("rad")
    my_ell = lax.axis_index("ell")
    barrier = pltpu.get_barrier_semaphore()
    for s in range(1, n):
        pl.semaphore_signal(barrier, inc=1, device_id={"rad": flipped(me, s, n)}, device_id_type=MESH)
    for s in range(1, n_ell):
        pl.semaphore_signal(barrier, inc=1, device_id={"ell": lax.rem(my_ell + s, n_ell)}, device_id_type=MESH)

    rows = pl.ds(pl.multiple_of(me * depth, depth), depth)
    locals_ = []
    for e in range(own):
        copy = pltpu.make_async_copy(fp_ref.at[me * own + e], held.at[e, rows], local_sem.at[e])
        copy.start()
        locals_.append(copy)
    pl.semaphore_wait(barrier, n - 1 + n_ell - 1)

    sends = []
    for e in range(own):
        chunk = []
        for s in range(n - 1, 0, -1):
            peer = flipped(me, s, n)
            copy = pltpu.make_async_remote_copy(
                src_ref=fp_ref.at[peer * own + e],
                dst_ref=held.at[e, rows],
                send_sem=send_sem.at[e, s],
                recv_sem=recv_sem.at[e, s],
                device_id={"rad": peer},
                device_id_type=MESH,
            )
            copy.start()
            chunk.append(copy)
        sends.append(chunk)

    slots = lax.broadcasted_iota(jnp.int32, (m_size, n_size), 0)
    for e in range(own):
        locals_[e].wait()
        for copy in sends[e]:
            copy.wait_recv()
        coef = lax.dot_general(
            held[e, :, :m_size], held[e, :, m_size:], (((0,), (0,)), ((), ())),
            preferred_element_type=jnp.float32,
        )
        valid = slots < 2 * ell_ref[me * own + e] + 1
        coef = jnp.where(valid, coef, 0.0)
        mine[e : e + 1, :] = jnp.sum(coef * coef, axis=0, keepdims=True)
        mine[own + e : own + e + 1, :] = jnp.max(jnp.abs(coef), axis=0, keepdims=True)

    copies = []
    for s in range(n - 1, 0, -1):
        copy = pltpu.make_async_remote_copy(
            src_ref=mine, dst_ref=stats.at[me], send_sem=send2.at[s], recv_sem=recv2.at[s],
            device_id={"rad": flipped(me, s, n)}, device_id_type=MESH,
        )
        copy.start()
        copies.append(copy)
    stats[me] = mine[...]
    for copy in copies:
        copy.wait_recv()
    every = stats[...]
    column = jnp.zeros((1, n_size), jnp.float32)
    top = jnp.zeros((1, n_size), jnp.float32)
    for s in range(n):
        energy_ref[s * own : (s + 1) * own, :] = every[s, :own]
        peak_ref[s * own : (s + 1) * own, :] = every[s, own:]
        column = column + jnp.sum(every[s, :own], axis=0, keepdims=True)
        top = jnp.maximum(top, jnp.max(every[s, own:], axis=0, keepdims=True))
    mine2[0:1, :] = column
    mine2[1:2, :] = top
    others = []
    for s in range(1, n_ell):
        copy = pltpu.make_async_remote_copy(
            src_ref=mine2, dst_ref=totals.at[my_ell], send_sem=send3.at[s], recv_sem=recv3.at[s],
            device_id={"ell": lax.rem(my_ell + s, n_ell)}, device_id_type=MESH,
        )
        copy.start()
        others.append(copy)
    totals[my_ell] = mine2[...]
    for copy in others:
        copy.wait_recv()
    both = totals[...]
    column = both[0, 0:1]
    top = both[0, 1:2]
    for s in range(1, n_ell):
        column = column + both[s, 0:1]
        top = jnp.maximum(top, both[s, 1:2])
    total_ref[0:1, :] = column
    total_ref[1:2, :] = top
    for chunk in sends:
        for copy in chunk:
            copy.wait_send()
    for copy in copies + others:
        copy.wait_send()


def by_ells(field, projection, ell_ids):
    n, n_ell = lax.axis_size("rad"), lax.axis_size("ell")
    depth, ells, m_size = field.shape
    n_size = projection.shape[2]
    own = ells // n
    fp = jnp.transpose(jnp.concatenate([field, projection], axis=2), (1, 0, 2))
    vmem = pl.BlockSpec(memory_space=pltpu.VMEM)
    energy, peak, total = pl.pallas_call(
        functools.partial(project_kernel, n, n_ell, own, depth, m_size, n_size),
        out_shape=(
            jax.ShapeDtypeStruct((ells, n_size), jnp.float32),
            jax.ShapeDtypeStruct((ells, n_size), jnp.float32),
            jax.ShapeDtypeStruct((2, n_size), jnp.float32),
        ),
        in_specs=[pl.BlockSpec(memory_space=pltpu.SMEM), pl.BlockSpec(memory_space=pl.ANY)],
        out_specs=(vmem, vmem, vmem),
        scratch_shapes=[
            pltpu.VMEM((own, n * depth, m_size + n_size), jnp.bfloat16),
            pltpu.VMEM((2 * own, n_size), jnp.float32),
            pltpu.VMEM((n, 2 * own, n_size), jnp.float32),
            pltpu.VMEM((2, n_size), jnp.float32),
            pltpu.VMEM((n_ell, 2, n_size), jnp.float32),
            pltpu.SemaphoreType.DMA((own, n)),
            pltpu.SemaphoreType.DMA((own, n)),
            pltpu.SemaphoreType.DMA((own,)),
            pltpu.SemaphoreType.DMA((n,)),
            pltpu.SemaphoreType.DMA((n,)),
            pltpu.SemaphoreType.DMA((n_ell,)),
            pltpu.SemaphoreType.DMA((n_ell,)),
        ],
        compiler_params=pltpu.CompilerParams(collective_id=0, has_side_effects=True),
    )(ell_ids, fp)
    width = n_size // n
    start = lax.axis_index("rad") * width
    energy, peak, total = (lax.dynamic_slice_in_dim(a, start, width, axis=1) for a in (energy, peak, total))
    share = (ells * n_ell) * energy / (total[0:1] + 1e-06)
    crest = peak / (total[1:2] + 1e-06)
    return share, crest


def by_slots(field, projection, ell_ids):
    exchanged = lax.all_to_all(field, "rad", split_axis=2, concat_axis=0, tiled=True)
    slot_share = exchanged.shape[2]
    coef = jnp.einsum(
        "rem,ren->emn",
        exchanged,
        lax.all_gather(projection, "rad", axis=0, tiled=True),
        preferred_element_type=jnp.float32,
    )
    slots = lax.axis_index("rad") * slot_share + jnp.arange(slot_share, dtype=jnp.int32)
    valid = (slots[None, :] < 2 * ell_ids[:, None] + 1).astype(jnp.float32)
    energy_part = jnp.sum(valid[:, :, None] * coef * coef, axis=1)
    peak_part = jnp.max(valid[:, :, None] * jnp.abs(coef), axis=1)
    energy_all, peak_all = (
        lax.all_to_all(energy_part[None], "rad", split_axis=2, concat_axis=0, tiled=True),
        lax.all_to_all(peak_part[None], "rad", split_axis=2, concat_axis=0, tiled=True),
    )
    energy = jnp.sum(energy_all, axis=0)
    peak = jnp.max(peak_all, axis=0)
    column = lax.psum(jnp.sum(energy, axis=0), "ell") + 1e-06
    top = lax.pmax(jnp.max(peak, axis=0), "ell") + 1e-06
    total_ells = ell_ids.shape[0] * lax.axis_size("ell")
    share = total_ells * energy / column[None, :]
    crest = peak / top[None, :]
    return (share, crest)


def per_device(field, projection, ell_ids):
    n = lax.axis_size("rad")
    depth, ells, _ = field.shape
    if ells % n == 0 and n & (n - 1) == 0 and depth % 16 == 0:
        return by_ells(field, projection, ell_ids)
    return by_slots(field, projection, ell_ids)


def solution(mesh):
    in_specs = (P("rad", "ell", None), P("rad", "ell", None), P("ell"))
    out_specs = (P("ell", "rad"), P("ell", "rad"))
    return jax.shard_map(
        per_device, mesh=mesh, in_specs=in_specs, out_specs=out_specs, check_vma=False
    )
```

```python
import functools

import jax
import jax.numpy as jnp
from jax import lax
from jax.experimental import pallas as pl
from jax.experimental.pallas import tpu as pltpu
from jax.sharding import PartitionSpec as P

MESH = pl.DeviceIdType.MESH


def flipped(me, step, n):
    peer, bit = 0, 1
    while bit < n:
        b = (me // bit) % 2
        peer = peer + bit * ((1 - b) if step & bit else b)
        bit *= 2
    return peer


def project_kernel(n, n_ell, own, depth, m_size, n_size, ell_ref, f_ref, p_ref, share_ref, crest_ref,
                   held_f, held_p, mine, stats, mine2, totals,
                   send_sem, recv_sem, local_sem, send2, recv2, send3, recv3):
    me = lax.axis_index("rad")
    my_ell = lax.axis_index("ell")
    barrier = pltpu.get_barrier_semaphore()
    for s in range(1, n):
        pl.semaphore_signal(barrier, inc=1, device_id={"rad": flipped(me, s, n)}, device_id_type=MESH)
    for s in range(1, n_ell):
        pl.semaphore_signal(barrier, inc=1, device_id={"ell": lax.rem(my_ell + s, n_ell)}, device_id_type=MESH)

    rows = pl.ds(pl.multiple_of(me * depth, depth), depth)
    locals_ = []
    for e in range(own):
        for i, (src, held) in enumerate(((f_ref, held_f), (p_ref, held_p))):
            copy = pltpu.make_async_copy(src.at[me * own + e], held.at[e, rows], local_sem.at[i, e])
            copy.start()
            locals_.append(copy)
    pl.semaphore_wait(barrier, n - 1 + n_ell - 1)

    sends = [[] for _ in range(own)]
    half = n // 2
    for steps in (range(half - 1, 0, -1), range(n - 1, half - 1, -1)):
        for e in range(own):
            for s in steps:
                peer = flipped(me, s, n)
                for i, (src, held) in enumerate(((p_ref, held_p), (f_ref, held_f))):
                    copy = pltpu.make_async_remote_copy(
                        src_ref=src.at[peer * own + e],
                        dst_ref=held.at[e, rows],
                        send_sem=send_sem.at[i, e, s],
                        recv_sem=recv_sem.at[i, e, s],
                        device_id={"rad": peer},
                        device_id_type=MESH,
                    )
                    copy.start()
                    sends[e].append(copy)

    slots = lax.broadcasted_iota(jnp.int32, (m_size, n_size), 0)
    for e in range(own):
        locals_[2 * e].wait()
        locals_[2 * e + 1].wait()
        for copy in sends[e]:
            copy.wait_recv()
        coef = lax.dot_general(
            held_f[e], held_p[e], (((0,), (0,)), ((), ())),
            preferred_element_type=jnp.float32,
        )
        valid = slots < 2 * ell_ref[me * own + e] + 1
        coef = jnp.where(valid, coef, 0.0)
        mine[e : e + 1, :] = jnp.sum(coef * coef, axis=0, keepdims=True)
        mine[own + e : own + e + 1, :] = jnp.max(jnp.abs(coef), axis=0, keepdims=True)

    copies = []
    for s in range(n - 1, 0, -1):
        copy = pltpu.make_async_remote_copy(
            src_ref=mine, dst_ref=stats.at[me], send_sem=send2.at[s], recv_sem=recv2.at[s],
            device_id={"rad": flipped(me, s, n)}, device_id_type=MESH,
        )
        copy.start()
        copies.append(copy)
    stats[me] = mine[...]
    for copy in copies:
        copy.wait_recv()
    every = stats[...]
    column = jnp.zeros((1, n_size), jnp.float32)
    top = jnp.zeros((1, n_size), jnp.float32)
    for s in range(n):
        column = column + jnp.sum(every[s, :own], axis=0, keepdims=True)
        top = jnp.maximum(top, jnp.max(every[s, own:], axis=0, keepdims=True))
    mine2[0:1, :] = column
    mine2[1:2, :] = top
    others = []
    for s in range(1, n_ell):
        copy = pltpu.make_async_remote_copy(
            src_ref=mine2, dst_ref=totals.at[my_ell], send_sem=send3.at[s], recv_sem=recv3.at[s],
            device_id={"ell": lax.rem(my_ell + s, n_ell)}, device_id_type=MESH,
        )
        copy.start()
        others.append(copy)
    totals[my_ell] = mine2[...]
    for copy in others:
        copy.wait_recv()
    both = totals[...]
    column = both[0, 0:1]
    top = both[0, 1:2]
    for s in range(1, n_ell):
        column = column + both[s, 0:1]
        top = jnp.maximum(top, both[s, 1:2])
    column = column + 1e-06
    top = top + 1e-06
    for s in range(n):
        share_ref[s * own : (s + 1) * own, :] = (n * own * n_ell) * every[s, :own] / column
        crest_ref[s * own : (s + 1) * own, :] = every[s, own:] / top
    for chunk in sends:
        for copy in chunk:
            copy.wait_send()
    for copy in copies + others:
        copy.wait_send()


def by_ells(field, projection, ell_ids):
    n, n_ell = lax.axis_size("rad"), lax.axis_size("ell")
    depth, ells, m_size = field.shape
    n_size = projection.shape[2]
    own = ells // n
    vmem = pl.BlockSpec(memory_space=pltpu.VMEM)
    share, crest = pl.pallas_call(
        functools.partial(project_kernel, n, n_ell, own, depth, m_size, n_size),
        out_shape=(
            jax.ShapeDtypeStruct((ells, n_size), jnp.float32),
            jax.ShapeDtypeStruct((ells, n_size), jnp.float32),
        ),
        in_specs=[pl.BlockSpec(memory_space=pltpu.SMEM)] + [pl.BlockSpec(memory_space=pl.ANY)] * 2,
        out_specs=(vmem, vmem),
        scratch_shapes=[
            pltpu.VMEM((own, n * depth, m_size), jnp.bfloat16),
            pltpu.VMEM((own, n * depth, n_size), jnp.bfloat16),
            pltpu.VMEM((2 * own, n_size), jnp.float32),
            pltpu.VMEM((n, 2 * own, n_size), jnp.float32),
            pltpu.VMEM((2, n_size), jnp.float32),
            pltpu.VMEM((n_ell, 2, n_size), jnp.float32),
            pltpu.SemaphoreType.DMA((2, own, n)),
            pltpu.SemaphoreType.DMA((2, own, n)),
            pltpu.SemaphoreType.DMA((2, own)),
            pltpu.SemaphoreType.DMA((n,)),
            pltpu.SemaphoreType.DMA((n,)),
            pltpu.SemaphoreType.DMA((n_ell,)),
            pltpu.SemaphoreType.DMA((n_ell,)),
        ],
        compiler_params=pltpu.CompilerParams(collective_id=0, has_side_effects=True),
    )(ell_ids, jnp.transpose(field, (1, 0, 2)), jnp.transpose(projection, (1, 0, 2)))
    width = n_size // n
    start = lax.axis_index("rad") * width
    return tuple(lax.dynamic_slice_in_dim(a, start, width, axis=1) for a in (share, crest))


def by_slots(field, projection, ell_ids):
    exchanged = lax.all_to_all(field, "rad", split_axis=2, concat_axis=0, tiled=True)
    slot_share = exchanged.shape[2]
    coef = jnp.einsum(
        "rem,ren->emn",
        exchanged,
        lax.all_gather(projection, "rad", axis=0, tiled=True),
        preferred_element_type=jnp.float32,
    )
    slots = lax.axis_index("rad") * slot_share + jnp.arange(slot_share, dtype=jnp.int32)
    valid = (slots[None, :] < 2 * ell_ids[:, None] + 1).astype(jnp.float32)
    energy_part = jnp.sum(valid[:, :, None] * coef * coef, axis=1)
    peak_part = jnp.max(valid[:, :, None] * jnp.abs(coef), axis=1)
    energy_all, peak_all = (
        lax.all_to_all(energy_part[None], "rad", split_axis=2, concat_axis=0, tiled=True),
        lax.all_to_all(peak_part[None], "rad", split_axis=2, concat_axis=0, tiled=True),
    )
    energy = jnp.sum(energy_all, axis=0)
    peak = jnp.max(peak_all, axis=0)
    column = lax.psum(jnp.sum(energy, axis=0), "ell") + 1e-06
    top = lax.pmax(jnp.max(peak, axis=0), "ell") + 1e-06
    total_ells = ell_ids.shape[0] * lax.axis_size("ell")
    share = total_ells * energy / column[None, :]
    crest = peak / top[None, :]
    return (share, crest)


def per_device(field, projection, ell_ids):
    n = lax.axis_size("rad")
    depth, ells, _ = field.shape
    if ells % n == 0 and n & (n - 1) == 0 and depth % 16 == 0:
        return by_ells(field, projection, ell_ids)
    return by_slots(field, projection, ell_ids)


def solution(mesh):
    in_specs = (P("rad", "ell", None), P("rad", "ell", None), P("ell"))
    out_specs = (P("ell", "rad"), P("ell", "rad"))
    return jax.shard_map(
        per_device, mesh=mesh, in_specs=in_specs, out_specs=out_specs, check_vma=False
    )
```

```python
import functools

import jax
import jax.numpy as jnp
from jax import lax
from jax.experimental import pallas as pl
from jax.experimental.pallas import tpu as pltpu
from jax.sharding import PartitionSpec as P

MESH = pl.DeviceIdType.MESH


def flipped(me, step, n):
    peer, bit = 0, 1
    while bit < n:
        b = (me // bit) % 2
        peer = peer + bit * ((1 - b) if step & bit else b)
        bit *= 2
    return peer


def project_kernel(n, n_ell, own, depth, m_size, n_size, ell_ref, f_ref, p_ref, share_ref, crest_ref,
                   stage_f, stage_p, held_f, held_p, mine, stats, mine2, totals,
                   send_sem, recv_sem, local_sem, send2, recv2, send3, recv3):
    me = lax.axis_index("rad")
    my_ell = lax.axis_index("ell")
    barrier = pltpu.get_barrier_semaphore()
    for s in range(1, n):
        pl.semaphore_signal(barrier, inc=1, device_id={"rad": flipped(me, s, n)}, device_id_type=MESH)
    for s in range(1, n_ell):
        pl.semaphore_signal(barrier, inc=1, device_id={"ell": lax.rem(my_ell + s, n_ell)}, device_id_type=MESH)

    rows = pl.ds(pl.multiple_of(me * depth, depth), depth)
    pl.semaphore_wait(barrier, n - 1 + n_ell - 1)

    arrays = ((p_ref, stage_p, held_p), (f_ref, stage_f, held_f))

    def stage(e):
        for src, staged, _ in arrays:
            staged[e] = jnp.swapaxes(src[:, e * n : (e + 1) * n, :], 0, 1)

    locals_ = []
    sends = [[] for _ in range(own)]
    stage(0)
    for e in range(own):
        if e + 1 < own:
            stage(e + 1)
        for s in range(n - 1, 0, -1):
            peer = flipped(me, s, n)
            for i, (_, staged, held) in enumerate(arrays):
                copy = pltpu.make_async_remote_copy(
                    src_ref=staged.at[e, peer],
                    dst_ref=held.at[e, rows],
                    send_sem=send_sem.at[i, e, s],
                    recv_sem=recv_sem.at[i, e, s],
                    device_id={"rad": peer},
                    device_id_type=MESH,
                )
                copy.start()
                sends[e].append(copy)
        for i, (_, staged, held) in enumerate(arrays):
            copy = pltpu.make_async_copy(staged.at[e, me], held.at[e, rows], local_sem.at[i, e])
            copy.start()
            locals_.append(copy)

    slots = lax.broadcasted_iota(jnp.int32, (m_size, n_size), 0)
    for e in range(own):
        locals_[2 * e].wait()
        locals_[2 * e + 1].wait()
        for copy in sends[e]:
            copy.wait_recv()
        coef = lax.dot_general(
            held_f[e], held_p[e], (((0,), (0,)), ((), ())),
            preferred_element_type=jnp.float32,
        )
        valid = slots < 2 * ell_ref[e * n + me] + 1
        coef = jnp.where(valid, coef, 0.0)
        mine[e : e + 1, :] = jnp.sum(coef * coef, axis=0, keepdims=True)
        mine[own + e : own + e + 1, :] = jnp.max(jnp.abs(coef), axis=0, keepdims=True)

    copies = []
    for s in range(n - 1, 0, -1):
        copy = pltpu.make_async_remote_copy(
            src_ref=mine, dst_ref=stats.at[me], send_sem=send2.at[s], recv_sem=recv2.at[s],
            device_id={"rad": flipped(me, s, n)}, device_id_type=MESH,
        )
        copy.start()
        copies.append(copy)
    stats[me] = mine[...]
    for copy in copies:
        copy.wait_recv()
    every = stats[...]
    column = jnp.zeros((1, n_size), jnp.float32)
    top = jnp.zeros((1, n_size), jnp.float32)
    for s in range(n):
        column = column + jnp.sum(every[s, :own], axis=0, keepdims=True)
        top = jnp.maximum(top, jnp.max(every[s, own:], axis=0, keepdims=True))
    mine2[0:1, :] = column
    mine2[1:2, :] = top
    others = []
    for s in range(1, n_ell):
        copy = pltpu.make_async_remote_copy(
            src_ref=mine2, dst_ref=totals.at[my_ell], send_sem=send3.at[s], recv_sem=recv3.at[s],
            device_id={"ell": lax.rem(my_ell + s, n_ell)}, device_id_type=MESH,
        )
        copy.start()
        others.append(copy)
    totals[my_ell] = mine2[...]
    for copy in others:
        copy.wait_recv()
    both = totals[...]
    column = both[0, 0:1]
    top = both[0, 1:2]
    for s in range(1, n_ell):
        column = column + both[s, 0:1]
        top = jnp.maximum(top, both[s, 1:2])
    column = column + 1e-06
    top = top + 1e-06
    for e in range(own):
        for s in range(n):
            at = slice(e * n + s, e * n + s + 1)
            share_ref[at, :] = (n * own * n_ell) * every[s, e : e + 1] / column
            crest_ref[at, :] = every[s, own + e : own + e + 1] / top
    for chunk in sends:
        for copy in chunk:
            copy.wait_send()
    for copy in copies + others:
        copy.wait_send()


def by_ells(field, projection, ell_ids):
    n, n_ell = lax.axis_size("rad"), lax.axis_size("ell")
    depth, ells, m_size = field.shape
    n_size = projection.shape[2]
    own = ells // n
    vmem = pl.BlockSpec(memory_space=pltpu.VMEM)
    share, crest = pl.pallas_call(
        functools.partial(project_kernel, n, n_ell, own, depth, m_size, n_size),
        out_shape=(
            jax.ShapeDtypeStruct((ells, n_size), jnp.float32),
            jax.ShapeDtypeStruct((ells, n_size), jnp.float32),
        ),
        in_specs=[pl.BlockSpec(memory_space=pltpu.SMEM)] + [vmem] * 2,
        out_specs=(vmem, vmem),
        scratch_shapes=[
            pltpu.VMEM((own, n, depth, m_size), jnp.bfloat16),
            pltpu.VMEM((own, n, depth, n_size), jnp.bfloat16),
            pltpu.VMEM((own, n * depth, m_size), jnp.bfloat16),
            pltpu.VMEM((own, n * depth, n_size), jnp.bfloat16),
            pltpu.VMEM((2 * own, n_size), jnp.float32),
            pltpu.VMEM((n, 2 * own, n_size), jnp.float32),
            pltpu.VMEM((2, n_size), jnp.float32),
            pltpu.VMEM((n_ell, 2, n_size), jnp.float32),
            pltpu.SemaphoreType.DMA((2, own, n)),
            pltpu.SemaphoreType.DMA((2, own, n)),
            pltpu.SemaphoreType.DMA((2, own)),
            pltpu.SemaphoreType.DMA((n,)),
            pltpu.SemaphoreType.DMA((n,)),
            pltpu.SemaphoreType.DMA((n_ell,)),
            pltpu.SemaphoreType.DMA((n_ell,)),
        ],
        compiler_params=pltpu.CompilerParams(collective_id=0, has_side_effects=True),
    )(ell_ids, field, projection)
    width = n_size // n
    start = lax.axis_index("rad") * width
    return tuple(lax.dynamic_slice_in_dim(a, start, width, axis=1) for a in (share, crest))


def by_slots(field, projection, ell_ids):
    exchanged = lax.all_to_all(field, "rad", split_axis=2, concat_axis=0, tiled=True)
    slot_share = exchanged.shape[2]
    coef = jnp.einsum(
        "rem,ren->emn",
        exchanged,
        lax.all_gather(projection, "rad", axis=0, tiled=True),
        preferred_element_type=jnp.float32,
    )
    slots = lax.axis_index("rad") * slot_share + jnp.arange(slot_share, dtype=jnp.int32)
    valid = (slots[None, :] < 2 * ell_ids[:, None] + 1).astype(jnp.float32)
    energy_part = jnp.sum(valid[:, :, None] * coef * coef, axis=1)
    peak_part = jnp.max(valid[:, :, None] * jnp.abs(coef), axis=1)
    energy_all, peak_all = (
        lax.all_to_all(energy_part[None], "rad", split_axis=2, concat_axis=0, tiled=True),
        lax.all_to_all(peak_part[None], "rad", split_axis=2, concat_axis=0, tiled=True),
    )
    energy = jnp.sum(energy_all, axis=0)
    peak = jnp.max(peak_all, axis=0)
    column = lax.psum(jnp.sum(energy, axis=0), "ell") + 1e-06
    top = lax.pmax(jnp.max(peak, axis=0), "ell") + 1e-06
    total_ells = ell_ids.shape[0] * lax.axis_size("ell")
    share = total_ells * energy / column[None, :]
    crest = peak / top[None, :]
    return (share, crest)


def per_device(field, projection, ell_ids):
    n = lax.axis_size("rad")
    depth, ells, _ = field.shape
    if ells % n == 0 and n % 8 == 0 and n & (n - 1) == 0 and depth % 16 == 0:
        return by_ells(field, projection, ell_ids)
    return by_slots(field, projection, ell_ids)


def solution(mesh):
    in_specs = (P("rad", "ell", None), P("rad", "ell", None), P("ell"))
    out_specs = (P("ell", "rad"), P("ell", "rad"))
    return jax.shard_map(
        per_device, mesh=mesh, in_specs=in_specs, out_specs=out_specs, check_vma=False
    )
```

```python
import functools

import jax
import jax.numpy as jnp
from jax import lax
from jax.experimental import pallas as pl
from jax.experimental.pallas import tpu as pltpu
from jax.sharding import PartitionSpec as P

MESH = pl.DeviceIdType.MESH


def flipped(me, step, n):
    peer, bit = 0, 1
    while bit < n:
        b = (me // bit) % 2
        peer = peer + bit * ((1 - b) if step & bit else b)
        bit *= 2
    return peer


def project_kernel(n, n_ell, own, depth, m_size, n_size, cut, ell_ref, f_ref, p_ref, share_ref, crest_ref,
                   stage_f, stage_p, held_f, held_p, mine, stats, mine2, totals,
                   relay_f, relay_p,
                   send_sem, recv_sem, local_sem, relay_sem, relay_send, send2, recv2, send3, recv3):
    me = lax.axis_index("rad")
    my_ell = lax.axis_index("ell")
    barrier = pltpu.get_barrier_semaphore()
    for s in range(1, n):
        pl.semaphore_signal(barrier, inc=1, device_id={"rad": flipped(me, s, n)}, device_id_type=MESH)
    for s in range(1, n_ell):
        pl.semaphore_signal(barrier, inc=1, device_id={"ell": lax.rem(my_ell + s, n_ell)}, device_id_type=MESH)

    shift, half = n_ell // 2, n // 2
    across = flipped(me, half, n)
    greeted = n - 1 + n_ell - 1
    if cut < m_size:
        pl.semaphore_signal(
            barrier, inc=1, device_id={"rad": across, "ell": lax.rem(my_ell + shift, n_ell)}, device_id_type=MESH
        )
        greeted += 1
    rows = pl.ds(pl.multiple_of(me * depth, depth), depth)
    pl.semaphore_wait(barrier, greeted)

    def main(role):
        width = cut if role == 1 else m_size
        arrays = (
            (p_ref, stage_p, held_p, relay_p, n_size),
            (f_ref, stage_f, held_f, relay_f, width),
        )
        relayed = [(0, 0), (1, 0), (0, 1)] if role else []

        def stage(e):
            for src, staged, _, _, w in arrays:
                staged[e, :, :, :w] = jnp.swapaxes(src[:, e * n : (e + 1) * n, :w], 0, 1)

        def send(i, e, s):
            _, staged, held, _, w = arrays[i]
            peer = flipped(me, s, n)
            return pltpu.make_async_remote_copy(
                src_ref=staged.at[e, peer, :, pl.ds(0, w)],
                dst_ref=held.at[e, rows, pl.ds(0, w)],
                send_sem=send_sem.at[i, e, s],
                recv_sem=recv_sem.at[i, e, s],
                device_id={"rad": peer},
                device_id_type=MESH,
            )

        def to_relay(k):
            i, e = relayed[k]
            _, staged, _, relay, _ = arrays[i]
            return pltpu.make_async_remote_copy(
                src_ref=staged.at[e, across],
                dst_ref=relay.at[e],
                send_sem=send_sem.at[i, e, half],
                recv_sem=relay_sem.at[k],
                device_id={"ell": lax.rem(my_ell + shift, n_ell)},
                device_id_type=MESH,
            )

        def from_relay(k):
            i, e = relayed[k]
            _, _, held, relay, _ = arrays[i]
            return pltpu.make_async_remote_copy(
                src_ref=relay.at[e],
                dst_ref=held.at[e, rows],
                send_sem=relay_send.at[k],
                recv_sem=recv_sem.at[i, e, half],
                device_id={"rad": across, "ell": lax.rem(my_ell + shift, n_ell)},
                device_id_type=MESH,
            )

        locals_ = []
        arrivals = [[] for _ in range(own)]
        waits = []
        stage(0)
        for e in range(own):
            if e + 1 < own:
                stage(e + 1)
            if role == 2:
                for k, (i, at) in enumerate(relayed):
                    if at == e:
                        copy = to_relay(k)
                        copy.start()
                        waits.append(copy)
                        arrivals[e].append(from_relay(k))
            for s in range(n - 1, 0, -1):
                for i in range(2):
                    if role == 2 and s == half and (i, e) in relayed:
                        continue
                    copy = send(i, e, s)
                    copy.start()
                    waits.append(copy)
                    arrivals[e].append(copy)
            for i, (_, staged, held, _, w) in enumerate(arrays):
                copy = pltpu.make_async_copy(
                    staged.at[e, me, :, pl.ds(0, w)], held.at[e, rows, pl.ds(0, w)], local_sem.at[i, e]
                )
                copy.start()
                locals_.append(copy)
            if role == 1 and e == 1:
                for k in range(len(relayed)):
                    to_relay(k).wait_recv()
                    copy = from_relay(k)
                    copy.start()
                    waits.append(copy)

        slots = lax.broadcasted_iota(jnp.int32, (width, n_size), 0)
        for e in range(own):
            locals_[2 * e].wait()
            locals_[2 * e + 1].wait()
            for copy in arrivals[e]:
                copy.wait_recv()
            coef = lax.dot_general(
                held_f[e, :, :width], held_p[e], (((0,), (0,)), ((), ())),
                preferred_element_type=jnp.float32,
            )
            valid = slots < 2 * ell_ref[e * n + me] + 1
            coef = jnp.where(valid, coef, 0.0)
            mine[e : e + 1, :] = jnp.sum(coef * coef, axis=0, keepdims=True)
            mine[own + e : own + e + 1, :] = jnp.max(jnp.abs(coef), axis=0, keepdims=True)
        for copy in waits:
            copy.wait_send()

    if cut < m_size:
        pl.when(my_ell < shift)(functools.partial(main, 1))
        pl.when(my_ell >= shift)(functools.partial(main, 2))
    else:
        main(0)

    copies = []
    for s in range(n - 1, 0, -1):
        copy = pltpu.make_async_remote_copy(
            src_ref=mine, dst_ref=stats.at[me], send_sem=send2.at[s], recv_sem=recv2.at[s],
            device_id={"rad": flipped(me, s, n)}, device_id_type=MESH,
        )
        copy.start()
        copies.append(copy)
    stats[me] = mine[...]
    for copy in copies:
        copy.wait_recv()
    every = stats[...]
    column = jnp.zeros((1, n_size), jnp.float32)
    top = jnp.zeros((1, n_size), jnp.float32)
    for s in range(n):
        column = column + jnp.sum(every[s, :own], axis=0, keepdims=True)
        top = jnp.maximum(top, jnp.max(every[s, own:], axis=0, keepdims=True))
    mine2[0:1, :] = column
    mine2[1:2, :] = top
    others = []
    for s in range(1, n_ell):
        copy = pltpu.make_async_remote_copy(
            src_ref=mine2, dst_ref=totals.at[my_ell], send_sem=send3.at[s], recv_sem=recv3.at[s],
            device_id={"ell": lax.rem(my_ell + s, n_ell)}, device_id_type=MESH,
        )
        copy.start()
        others.append(copy)
    totals[my_ell] = mine2[...]
    for copy in others:
        copy.wait_recv()
    both = totals[...]
    column = both[0, 0:1]
    top = both[0, 1:2]
    for s in range(1, n_ell):
        column = column + both[s, 0:1]
        top = jnp.maximum(top, both[s, 1:2])
    column = column + 1e-06
    top = top + 1e-06
    for e in range(own):
        for s in range(n):
            at = slice(e * n + s, e * n + s + 1)
            share_ref[at, :] = (n * own * n_ell) * every[s, e : e + 1] / column
            crest_ref[at, :] = every[s, own + e : own + e + 1] / top
    for copy in copies + others:
        copy.wait_send()


def by_ells(field, projection, ell_ids):
    n, n_ell = lax.axis_size("rad"), lax.axis_size("ell")
    depth, ells, m_size = field.shape
    n_size = projection.shape[2]
    own = ells // n
    most = m_size // 2 - 1 - (ells * n_ell - ells * (n_ell // 2))
    cut = min(m_size, -(-(2 * most + 1) // 128) * 128)
    if n_ell % 2 or own < 2 or cut < 128:
        cut = m_size
    vmem = pl.BlockSpec(memory_space=pltpu.VMEM)
    share, crest = pl.pallas_call(
        functools.partial(project_kernel, n, n_ell, own, depth, m_size, n_size, cut),
        out_shape=(
            jax.ShapeDtypeStruct((ells, n_size), jnp.float32),
            jax.ShapeDtypeStruct((ells, n_size), jnp.float32),
        ),
        in_specs=[pl.BlockSpec(memory_space=pltpu.SMEM)] + [vmem] * 2,
        out_specs=(vmem, vmem),
        scratch_shapes=[
            pltpu.VMEM((own, n, depth, m_size), jnp.bfloat16),
            pltpu.VMEM((own, n, depth, n_size), jnp.bfloat16),
            pltpu.VMEM((own, n * depth, m_size), jnp.bfloat16),
            pltpu.VMEM((own, n * depth, n_size), jnp.bfloat16),
            pltpu.VMEM((2 * own, n_size), jnp.float32),
            pltpu.VMEM((n, 2 * own, n_size), jnp.float32),
            pltpu.VMEM((2, n_size), jnp.float32),
            pltpu.VMEM((n_ell, 2, n_size), jnp.float32),
            pltpu.VMEM((2, depth, m_size), jnp.bfloat16),
            pltpu.VMEM((2, depth, n_size), jnp.bfloat16),
            pltpu.SemaphoreType.DMA((2, own, n)),
            pltpu.SemaphoreType.DMA((2, own, n)),
            pltpu.SemaphoreType.DMA((2, own)),
            pltpu.SemaphoreType.DMA((3,)),
            pltpu.SemaphoreType.DMA((3,)),
            pltpu.SemaphoreType.DMA((n,)),
            pltpu.SemaphoreType.DMA((n,)),
            pltpu.SemaphoreType.DMA((n_ell,)),
            pltpu.SemaphoreType.DMA((n_ell,)),
        ],
        compiler_params=pltpu.CompilerParams(collective_id=0, has_side_effects=True),
    )(ell_ids, field, projection)
    width = n_size // n
    start = lax.axis_index("rad") * width
    return tuple(lax.dynamic_slice_in_dim(a, start, width, axis=1) for a in (share, crest))


def by_slots(field, projection, ell_ids):
    exchanged = lax.all_to_all(field, "rad", split_axis=2, concat_axis=0, tiled=True)
    slot_share = exchanged.shape[2]
    coef = jnp.einsum(
        "rem,ren->emn",
        exchanged,
        lax.all_gather(projection, "rad", axis=0, tiled=True),
        preferred_element_type=jnp.float32,
    )
    slots = lax.axis_index("rad") * slot_share + jnp.arange(slot_share, dtype=jnp.int32)
    valid = (slots[None, :] < 2 * ell_ids[:, None] + 1).astype(jnp.float32)
    energy_part = jnp.sum(valid[:, :, None] * coef * coef, axis=1)
    peak_part = jnp.max(valid[:, :, None] * jnp.abs(coef), axis=1)
    energy_all, peak_all = (
        lax.all_to_all(energy_part[None], "rad", split_axis=2, concat_axis=0, tiled=True),
        lax.all_to_all(peak_part[None], "rad", split_axis=2, concat_axis=0, tiled=True),
    )
    energy = jnp.sum(energy_all, axis=0)
    peak = jnp.max(peak_all, axis=0)
    column = lax.psum(jnp.sum(energy, axis=0), "ell") + 1e-06
    top = lax.pmax(jnp.max(peak, axis=0), "ell") + 1e-06
    total_ells = ell_ids.shape[0] * lax.axis_size("ell")
    share = total_ells * energy / column[None, :]
    crest = peak / top[None, :]
    return (share, crest)


def per_device(field, projection, ell_ids):
    n = lax.axis_size("rad")
    depth, ells, _ = field.shape
    if ells % n == 0 and n % 8 == 0 and n & (n - 1) == 0 and depth % 16 == 0:
        return by_ells(field, projection, ell_ids)
    return by_slots(field, projection, ell_ids)


def solution(mesh):
    in_specs = (P("rad", "ell", None), P("rad", "ell", None), P("ell"))
    out_specs = (P("ell", "rad"), P("ell", "rad"))
    return jax.shard_map(
        per_device, mesh=mesh, in_specs=in_specs, out_specs=out_specs, check_vma=False
    )
```

```python
import functools

import jax
import jax.numpy as jnp
from jax import lax
from jax.experimental import pallas as pl
from jax.experimental.pallas import tpu as pltpu
from jax.sharding import PartitionSpec as P

MESH = pl.DeviceIdType.MESH


def flipped(me, step, n):
    peer, bit = 0, 1
    while bit < n:
        b = (me // bit) % 2
        peer = peer + bit * ((1 - b) if step & bit else b)
        bit *= 2
    return peer


def project_kernel(n, n_ell, own, depth, m_size, n_size, cut, ell_ref, f_ref, p_ref, share_ref, crest_ref,
                   stage_f, stage_p, held_f, held_p, mine, stats, mine2, totals,
                   relay_f, relay_p,
                   send_sem, recv_sem, local_sem, relay_sem, relay_send, send2, recv2, send3, recv3):
    me = lax.axis_index("rad")
    my_ell = lax.axis_index("ell")
    barrier = pltpu.get_barrier_semaphore()
    for s in range(1, n):
        pl.semaphore_signal(barrier, inc=1, device_id={"rad": flipped(me, s, n)}, device_id_type=MESH)
    for s in range(1, n_ell):
        pl.semaphore_signal(barrier, inc=1, device_id={"ell": lax.rem(my_ell + s, n_ell)}, device_id_type=MESH)

    shift, half = n_ell // 2, n // 2
    across = flipped(me, half, n)
    greeted = n - 1 + n_ell - 1
    if cut < m_size:
        pl.semaphore_signal(
            barrier, inc=1, device_id={"rad": across, "ell": lax.rem(my_ell + shift, n_ell)}, device_id_type=MESH
        )
        greeted += 1
    rows = pl.ds(pl.multiple_of(me * depth, depth), depth)

    def main(role):
        width = cut if role == 1 else m_size
        arrays = (
            (p_ref, stage_p, held_p, relay_p, n_size),
            (f_ref, stage_f, held_f, relay_f, width),
        )
        relayed = [(0, 0), (1, 0), (0, 1)] if role else []

        def stage(e):
            for src, staged, _, _, w in arrays:
                staged[e, :, :, :w] = jnp.swapaxes(src[:, e * n : (e + 1) * n, :w], 0, 1)

        def send(i, e, s):
            _, staged, held, _, w = arrays[i]
            peer = flipped(me, s, n)
            return pltpu.make_async_remote_copy(
                src_ref=staged.at[e, peer, :, pl.ds(0, w)],
                dst_ref=held.at[e, rows, pl.ds(0, w)],
                send_sem=send_sem.at[i, e, s],
                recv_sem=recv_sem.at[i, e, s],
                device_id={"rad": peer},
                device_id_type=MESH,
            )

        def to_relay(k):
            i, e = relayed[k]
            _, staged, _, relay, _ = arrays[i]
            return pltpu.make_async_remote_copy(
                src_ref=staged.at[e, across],
                dst_ref=relay.at[e],
                send_sem=send_sem.at[i, e, half],
                recv_sem=relay_sem.at[k],
                device_id={"ell": lax.rem(my_ell + shift, n_ell)},
                device_id_type=MESH,
            )

        def from_relay(k):
            i, e = relayed[k]
            _, _, held, relay, _ = arrays[i]
            return pltpu.make_async_remote_copy(
                src_ref=relay.at[e],
                dst_ref=held.at[e, rows],
                send_sem=relay_send.at[k],
                recv_sem=recv_sem.at[i, e, half],
                device_id={"rad": across, "ell": lax.rem(my_ell + shift, n_ell)},
                device_id_type=MESH,
            )

        locals_ = []
        arrivals = [[] for _ in range(own)]
        waits = []
        stage(0)
        pl.semaphore_wait(barrier, greeted)
        for e in range(own):
            for later in range(1 if e == 1 else e + 1, min(e + 2, own) if e else 0):
                stage(later)
            if role == 2:
                for k, (i, at) in enumerate(relayed):
                    if at == e:
                        copy = to_relay(k)
                        copy.start()
                        waits.append(copy)
                        arrivals[e].append(from_relay(k))
            for s in range(n - 1, 0, -1):
                for i in range(2):
                    if role == 2 and s == half and (i, e) in relayed:
                        continue
                    copy = send(i, e, s)
                    copy.start()
                    waits.append(copy)
                    arrivals[e].append(copy)
            for i, (_, staged, held, _, w) in enumerate(arrays):
                copy = pltpu.make_async_copy(
                    staged.at[e, me, :, pl.ds(0, w)], held.at[e, rows, pl.ds(0, w)], local_sem.at[i, e]
                )
                copy.start()
                locals_.append(copy)
            if role == 1 and e == 1:
                for k in range(len(relayed)):
                    to_relay(k).wait_recv()
                    copy = from_relay(k)
                    copy.start()
                    waits.append(copy)

        slots = lax.broadcasted_iota(jnp.int32, (width, n_size), 0)
        for e in range(own):
            locals_[2 * e].wait()
            locals_[2 * e + 1].wait()
            for copy in arrivals[e]:
                copy.wait_recv()
            coef = lax.dot_general(
                held_f[e, :, :width], held_p[e], (((0,), (0,)), ((), ())),
                preferred_element_type=jnp.float32,
            )
            valid = slots < 2 * ell_ref[e * n + me] + 1
            coef = jnp.where(valid, coef, 0.0)
            mine[e : e + 1, :] = jnp.sum(coef * coef, axis=0, keepdims=True)
            mine[own + e : own + e + 1, :] = jnp.max(jnp.abs(coef), axis=0, keepdims=True)

        copies = []
        for s in range(n - 1, 0, -1):
            copy = pltpu.make_async_remote_copy(
                src_ref=mine, dst_ref=stats.at[me], send_sem=send2.at[s], recv_sem=recv2.at[s],
                device_id={"rad": flipped(me, s, n)}, device_id_type=MESH,
            )
            copy.start()
            copies.append(copy)
        stats[me] = mine[...]
        for copy in copies:
            copy.wait_recv()
        every = stats[...]
        column = jnp.zeros((1, n_size), jnp.float32)
        top = jnp.zeros((1, n_size), jnp.float32)
        for s in range(n):
            column = column + jnp.sum(every[s, :own], axis=0, keepdims=True)
            top = jnp.maximum(top, jnp.max(every[s, own:], axis=0, keepdims=True))
        mine2[0:1, :] = column
        mine2[1:2, :] = top
        others = []
        for s in range(1, n_ell):
            copy = pltpu.make_async_remote_copy(
                src_ref=mine2, dst_ref=totals.at[my_ell], send_sem=send3.at[s], recv_sem=recv3.at[s],
                device_id={"ell": lax.rem(my_ell + s, n_ell)}, device_id_type=MESH,
            )
            copy.start()
            others.append(copy)
        totals[my_ell] = mine2[...]
        for copy in others:
            copy.wait_recv()
        both = totals[...]
        column = both[0, 0:1]
        top = both[0, 1:2]
        for s in range(1, n_ell):
            column = column + both[s, 0:1]
            top = jnp.maximum(top, both[s, 1:2])
        column = column + 1e-06
        top = top + 1e-06
        for e in range(own):
            for s in range(n):
                at = slice(e * n + s, e * n + s + 1)
                share_ref[at, :] = (n * own * n_ell) * every[s, e : e + 1] / column
                crest_ref[at, :] = every[s, own + e : own + e + 1] / top
        for copy in copies + others:
            copy.wait_send()
        for copy in waits:
            copy.wait_send()

    if cut < m_size:
        pl.when(my_ell < shift)(functools.partial(main, 1))
        pl.when(my_ell >= shift)(functools.partial(main, 2))
    else:
        main(0)


def by_ells(field, projection, ell_ids):
    n, n_ell = lax.axis_size("rad"), lax.axis_size("ell")
    depth, ells, m_size = field.shape
    n_size = projection.shape[2]
    own = ells // n
    most = m_size // 2 - 1 - (ells * n_ell - ells * (n_ell // 2))
    cut = min(m_size, -(-(2 * most + 1) // 128) * 128)
    if n_ell % 2 or own < 2 or cut < 128:
        cut = m_size
    vmem = pl.BlockSpec(memory_space=pltpu.VMEM)
    share, crest = pl.pallas_call(
        functools.partial(project_kernel, n, n_ell, own, depth, m_size, n_size, cut),
        out_shape=(
            jax.ShapeDtypeStruct((ells, n_size), jnp.float32),
            jax.ShapeDtypeStruct((ells, n_size), jnp.float32),
        ),
        in_specs=[pl.BlockSpec(memory_space=pltpu.SMEM)] + [vmem] * 2,
        out_specs=(vmem, vmem),
        scratch_shapes=[
            pltpu.VMEM((own, n, depth, m_size), jnp.bfloat16),
            pltpu.VMEM((own, n, depth, n_size), jnp.bfloat16),
            pltpu.VMEM((own, n * depth, m_size), jnp.bfloat16),
            pltpu.VMEM((own, n * depth, n_size), jnp.bfloat16),
            pltpu.VMEM((2 * own, n_size), jnp.float32),
            pltpu.VMEM((n, 2 * own, n_size), jnp.float32),
            pltpu.VMEM((2, n_size), jnp.float32),
            pltpu.VMEM((n_ell, 2, n_size), jnp.float32),
            pltpu.VMEM((2, depth, m_size), jnp.bfloat16),
            pltpu.VMEM((2, depth, n_size), jnp.bfloat16),
            pltpu.SemaphoreType.DMA((2, own, n)),
            pltpu.SemaphoreType.DMA((2, own, n)),
            pltpu.SemaphoreType.DMA((2, own)),
            pltpu.SemaphoreType.DMA((3,)),
            pltpu.SemaphoreType.DMA((3,)),
            pltpu.SemaphoreType.DMA((n,)),
            pltpu.SemaphoreType.DMA((n,)),
            pltpu.SemaphoreType.DMA((n_ell,)),
            pltpu.SemaphoreType.DMA((n_ell,)),
        ],
        compiler_params=pltpu.CompilerParams(collective_id=0, has_side_effects=True),
    )(ell_ids, field, projection)
    width = n_size // n
    start = lax.axis_index("rad") * width
    return tuple(lax.dynamic_slice_in_dim(a, start, width, axis=1) for a in (share, crest))


def by_slots(field, projection, ell_ids):
    exchanged = lax.all_to_all(field, "rad", split_axis=2, concat_axis=0, tiled=True)
    slot_share = exchanged.shape[2]
    coef = jnp.einsum(
        "rem,ren->emn",
        exchanged,
        lax.all_gather(projection, "rad", axis=0, tiled=True),
        preferred_element_type=jnp.float32,
    )
    slots = lax.axis_index("rad") * slot_share + jnp.arange(slot_share, dtype=jnp.int32)
    valid = (slots[None, :] < 2 * ell_ids[:, None] + 1).astype(jnp.float32)
    energy_part = jnp.sum(valid[:, :, None] * coef * coef, axis=1)
    peak_part = jnp.max(valid[:, :, None] * jnp.abs(coef), axis=1)
    energy_all, peak_all = (
        lax.all_to_all(energy_part[None], "rad", split_axis=2, concat_axis=0, tiled=True),
        lax.all_to_all(peak_part[None], "rad", split_axis=2, concat_axis=0, tiled=True),
    )
    energy = jnp.sum(energy_all, axis=0)
    peak = jnp.max(peak_all, axis=0)
    column = lax.psum(jnp.sum(energy, axis=0), "ell") + 1e-06
    top = lax.pmax(jnp.max(peak, axis=0), "ell") + 1e-06
    total_ells = ell_ids.shape[0] * lax.axis_size("ell")
    share = total_ells * energy / column[None, :]
    crest = peak / top[None, :]
    return (share, crest)


def per_device(field, projection, ell_ids):
    n = lax.axis_size("rad")
    depth, ells, _ = field.shape
    if ells % n == 0 and n % 8 == 0 and n & (n - 1) == 0 and depth % 16 == 0:
        return by_ells(field, projection, ell_ids)
    return by_slots(field, projection, ell_ids)


def solution(mesh):
    in_specs = (P("rad", "ell", None), P("rad", "ell", None), P("ell"))
    out_specs = (P("ell", "rad"), P("ell", "rad"))
    return jax.shard_map(
        per_device, mesh=mesh, in_specs=in_specs, out_specs=out_specs, check_vma=False
    )
```

```python
import functools

import jax
import jax.numpy as jnp
from jax import lax
from jax.experimental import pallas as pl
from jax.experimental.pallas import tpu as pltpu
from jax.sharding import PartitionSpec as P

MESH = pl.DeviceIdType.MESH


def flipped(me, step, n):
    peer, bit = 0, 1
    while bit < n:
        b = (me // bit) % 2
        peer = peer + bit * ((1 - b) if step & bit else b)
        bit *= 2
    return peer


def project_kernel(n, n_ell, own, depth, m_size, n_size, cut, ell_ref, f_ref, p_ref, share_ref, crest_ref,
                   stage_f, stage_p, held_f, held_p, mine, stats, mine2, totals,
                   relay_f, relay_p,
                   send_sem, recv_sem, local_sem, relay_sem, relay_send, send2, recv2, send3, recv3):
    me = lax.axis_index("rad")
    my_ell = lax.axis_index("ell")
    barrier = pltpu.get_barrier_semaphore()
    for s in range(1, n):
        pl.semaphore_signal(barrier, inc=1, device_id={"rad": flipped(me, s, n)}, device_id_type=MESH)
    for s in range(1, n_ell):
        pl.semaphore_signal(barrier, inc=1, device_id={"ell": lax.rem(my_ell + s, n_ell)}, device_id_type=MESH)

    shift, half = n_ell // 2, n // 2
    across = flipped(me, half, n)
    greeted = n - 1 + n_ell - 1
    if cut < m_size:
        pl.semaphore_signal(
            barrier, inc=1, device_id={"rad": across, "ell": lax.rem(my_ell + shift, n_ell)}, device_id_type=MESH
        )
        greeted += 1
    rows = pl.ds(pl.multiple_of(me * depth, depth), depth)

    def main(role):
        width = cut if role == 1 else m_size
        arrays = (
            (p_ref, stage_p, held_p, relay_p, n_size),
            (f_ref, stage_f, held_f, relay_f, width),
        )
        relayed = [(0, 0), (1, 0), (0, 1)] if role else []

        def stage(e):
            for src, staged, _, _, w in arrays:
                staged[e, :, :, :w] = jnp.swapaxes(src[:, e * n : (e + 1) * n, :w], 0, 1)

        def send(i, e, s):
            _, staged, held, _, w = arrays[i]
            peer = flipped(me, s, n)
            return pltpu.make_async_remote_copy(
                src_ref=staged.at[e, peer, :, pl.ds(0, w)],
                dst_ref=held.at[e, rows, pl.ds(0, w)],
                send_sem=send_sem.at[i, e, s],
                recv_sem=recv_sem.at[i, e, s],
                device_id={"rad": peer},
                device_id_type=MESH,
            )

        def to_relay(k):
            i, e = relayed[k]
            _, staged, _, relay, _ = arrays[i]
            return pltpu.make_async_remote_copy(
                src_ref=staged.at[e, across],
                dst_ref=relay.at[e],
                send_sem=send_sem.at[i, e, half],
                recv_sem=relay_sem.at[k],
                device_id={"ell": lax.rem(my_ell + shift, n_ell)},
                device_id_type=MESH,
            )

        def from_relay(k):
            i, e = relayed[k]
            _, _, held, relay, _ = arrays[i]
            return pltpu.make_async_remote_copy(
                src_ref=relay.at[e],
                dst_ref=held.at[e, rows],
                send_sem=relay_send.at[k],
                recv_sem=recv_sem.at[i, e, half],
                device_id={"rad": across, "ell": lax.rem(my_ell + shift, n_ell)},
                device_id_type=MESH,
            )

        locals_ = []
        arrivals = [[] for _ in range(own)]
        waits = []
        stage(0)
        pl.semaphore_wait(barrier, greeted)
        near = list(range(half - 1, 0, -1))
        far = [half + at for pair in zip(range(half // 2, half), range(half // 2)) for at in pair]

        def start(e, steps):
            for s in steps:
                for i in range(2):
                    if role == 2 and s == half and (i, e) in relayed:
                        continue
                    copy = send(i, e, s)
                    copy.start()
                    waits.append(copy)
                    arrivals[e].append(copy)

        for e in range(own):
            if e == 1:
                for later in range(1, own):
                    stage(later)
                for later in range(1, own):
                    start(later, near)
            if role == 2:
                for k, (i, at) in enumerate(relayed):
                    if at == e:
                        copy = to_relay(k)
                        copy.start()
                        waits.append(copy)
                        arrivals[e].append(from_relay(k))
            if e == 0:
                start(e, near)
            start(e, far)
            for i, (_, staged, held, _, w) in enumerate(arrays):
                copy = pltpu.make_async_copy(
                    staged.at[e, me, :, pl.ds(0, w)], held.at[e, rows, pl.ds(0, w)], local_sem.at[i, e]
                )
                copy.start()
                locals_.append(copy)
            if role == 1 and e == 1:
                for k in range(len(relayed)):
                    to_relay(k).wait_recv()
                    copy = from_relay(k)
                    copy.start()
                    waits.append(copy)

        slots = lax.broadcasted_iota(jnp.int32, (width, n_size), 0)
        for e in range(own):
            locals_[2 * e].wait()
            locals_[2 * e + 1].wait()
            for copy in arrivals[e]:
                copy.wait_recv()
            coef = lax.dot_general(
                held_f[e, :, :width], held_p[e], (((0,), (0,)), ((), ())),
                preferred_element_type=jnp.float32,
            )
            valid = slots < 2 * ell_ref[e * n + me] + 1
            coef = jnp.where(valid, coef, 0.0)
            mine[e : e + 1, :] = jnp.sum(coef * coef, axis=0, keepdims=True)
            mine[own + e : own + e + 1, :] = jnp.max(jnp.abs(coef), axis=0, keepdims=True)

        copies = []
        for s in range(n - 1, 0, -1):
            copy = pltpu.make_async_remote_copy(
                src_ref=mine, dst_ref=stats.at[me], send_sem=send2.at[s], recv_sem=recv2.at[s],
                device_id={"rad": flipped(me, s, n)}, device_id_type=MESH,
            )
            copy.start()
            copies.append(copy)
        stats[me] = mine[...]
        for copy in copies:
            copy.wait_recv()
        every = stats[...]
        column = jnp.zeros((1, n_size), jnp.float32)
        top = jnp.zeros((1, n_size), jnp.float32)
        for s in range(n):
            column = column + jnp.sum(every[s, :own], axis=0, keepdims=True)
            top = jnp.maximum(top, jnp.max(every[s, own:], axis=0, keepdims=True))
        mine2[0:1, :] = column
        mine2[1:2, :] = top
        others = []
        for s in range(1, n_ell):
            copy = pltpu.make_async_remote_copy(
                src_ref=mine2, dst_ref=totals.at[my_ell], send_sem=send3.at[s], recv_sem=recv3.at[s],
                device_id={"ell": lax.rem(my_ell + s, n_ell)}, device_id_type=MESH,
            )
            copy.start()
            others.append(copy)
        totals[my_ell] = mine2[...]
        for copy in others:
            copy.wait_recv()
        both = totals[...]
        column = both[0, 0:1]
        top = both[0, 1:2]
        for s in range(1, n_ell):
            column = column + both[s, 0:1]
            top = jnp.maximum(top, both[s, 1:2])
        column = column + 1e-06
        top = top + 1e-06
        for e in range(own):
            for s in range(n):
                at = slice(e * n + s, e * n + s + 1)
                share_ref[at, :] = (n * own * n_ell) * every[s, e : e + 1] / column
                crest_ref[at, :] = every[s, own + e : own + e + 1] / top
        for copy in copies + others:
            copy.wait_send()
        for copy in waits:
            copy.wait_send()

    if cut < m_size:
        pl.when(my_ell < shift)(functools.partial(main, 1))
        pl.when(my_ell >= shift)(functools.partial(main, 2))
    else:
        main(0)


def by_ells(field, projection, ell_ids):
    n, n_ell = lax.axis_size("rad"), lax.axis_size("ell")
    depth, ells, m_size = field.shape
    n_size = projection.shape[2]
    own = ells // n
    most = m_size // 2 - 1 - (ells * n_ell - ells * (n_ell // 2))
    cut = min(m_size, -(-(2 * most + 1) // 128) * 128)
    if n_ell % 2 or own < 2 or cut < 128:
        cut = m_size
    vmem = pl.BlockSpec(memory_space=pltpu.VMEM)
    share, crest = pl.pallas_call(
        functools.partial(project_kernel, n, n_ell, own, depth, m_size, n_size, cut),
        out_shape=(
            jax.ShapeDtypeStruct((ells, n_size), jnp.float32),
            jax.ShapeDtypeStruct((ells, n_size), jnp.float32),
        ),
        in_specs=[pl.BlockSpec(memory_space=pltpu.SMEM)] + [vmem] * 2,
        out_specs=(vmem, vmem),
        scratch_shapes=[
            pltpu.VMEM((own, n, depth, m_size), jnp.bfloat16),
            pltpu.VMEM((own, n, depth, n_size), jnp.bfloat16),
            pltpu.VMEM((own, n * depth, m_size), jnp.bfloat16),
            pltpu.VMEM((own, n * depth, n_size), jnp.bfloat16),
            pltpu.VMEM((2 * own, n_size), jnp.float32),
            pltpu.VMEM((n, 2 * own, n_size), jnp.float32),
            pltpu.VMEM((2, n_size), jnp.float32),
            pltpu.VMEM((n_ell, 2, n_size), jnp.float32),
            pltpu.VMEM((2, depth, m_size), jnp.bfloat16),
            pltpu.VMEM((2, depth, n_size), jnp.bfloat16),
            pltpu.SemaphoreType.DMA((2, own, n)),
            pltpu.SemaphoreType.DMA((2, own, n)),
            pltpu.SemaphoreType.DMA((2, own)),
            pltpu.SemaphoreType.DMA((3,)),
            pltpu.SemaphoreType.DMA((3,)),
            pltpu.SemaphoreType.DMA((n,)),
            pltpu.SemaphoreType.DMA((n,)),
            pltpu.SemaphoreType.DMA((n_ell,)),
            pltpu.SemaphoreType.DMA((n_ell,)),
        ],
        compiler_params=pltpu.CompilerParams(collective_id=0, has_side_effects=True),
    )(ell_ids, field, projection)
    width = n_size // n
    start = lax.axis_index("rad") * width
    return tuple(lax.dynamic_slice_in_dim(a, start, width, axis=1) for a in (share, crest))


def by_slots(field, projection, ell_ids):
    exchanged = lax.all_to_all(field, "rad", split_axis=2, concat_axis=0, tiled=True)
    slot_share = exchanged.shape[2]
    coef = jnp.einsum(
        "rem,ren->emn",
        exchanged,
        lax.all_gather(projection, "rad", axis=0, tiled=True),
        preferred_element_type=jnp.float32,
    )
    slots = lax.axis_index("rad") * slot_share + jnp.arange(slot_share, dtype=jnp.int32)
    valid = (slots[None, :] < 2 * ell_ids[:, None] + 1).astype(jnp.float32)
    energy_part = jnp.sum(valid[:, :, None] * coef * coef, axis=1)
    peak_part = jnp.max(valid[:, :, None] * jnp.abs(coef), axis=1)
    energy_all, peak_all = (
        lax.all_to_all(energy_part[None], "rad", split_axis=2, concat_axis=0, tiled=True),
        lax.all_to_all(peak_part[None], "rad", split_axis=2, concat_axis=0, tiled=True),
    )
    energy = jnp.sum(energy_all, axis=0)
    peak = jnp.max(peak_all, axis=0)
    column = lax.psum(jnp.sum(energy, axis=0), "ell") + 1e-06
    top = lax.pmax(jnp.max(peak, axis=0), "ell") + 1e-06
    total_ells = ell_ids.shape[0] * lax.axis_size("ell")
    share = total_ells * energy / column[None, :]
    crest = peak / top[None, :]
    return (share, crest)


def per_device(field, projection, ell_ids):
    n = lax.axis_size("rad")
    depth, ells, _ = field.shape
    if ells % n == 0 and n % 8 == 0 and n & (n - 1) == 0 and depth % 16 == 0:
        return by_ells(field, projection, ell_ids)
    return by_slots(field, projection, ell_ids)


def solution(mesh):
    in_specs = (P("rad", "ell", None), P("rad", "ell", None), P("ell"))
    out_specs = (P("ell", "rad"), P("ell", "rad"))
    return jax.shard_map(
        per_device, mesh=mesh, in_specs=in_specs, out_specs=out_specs, check_vma=False
    )
```

```python
import functools

import jax
import jax.numpy as jnp
from jax import lax
from jax.experimental import pallas as pl
from jax.experimental.pallas import tpu as pltpu
from jax.sharding import PartitionSpec as P

MESH = pl.DeviceIdType.MESH


def flipped(me, step, n):
    peer, bit = 0, 1
    while bit < n:
        b = (me // bit) % 2
        peer = peer + bit * ((1 - b) if step & bit else b)
        bit *= 2
    return peer


def project_kernel(n, n_ell, own, depth, m_size, n_size, cut, ell_ref, f_hbm, p_hbm, share_ref, crest_ref,
                   f_ref, p_ref, fetch_sem, stage_f, stage_p, held_f, held_p, mine, stats, mine2, totals,
                   relay_f, relay_p,
                   send_sem, recv_sem, local_sem, relay_sem, relay_send, send2, recv2, send3, recv3):
    me = lax.axis_index("rad")
    my_ell = lax.axis_index("ell")
    barrier = pltpu.get_barrier_semaphore()
    for s in range(1, n):
        pl.semaphore_signal(barrier, inc=1, device_id={"rad": flipped(me, s, n)}, device_id_type=MESH)
    for s in range(1, n_ell):
        pl.semaphore_signal(barrier, inc=1, device_id={"ell": lax.rem(my_ell + s, n_ell)}, device_id_type=MESH)

    shift, half = n_ell // 2, n // 2
    across = flipped(me, half, n)
    greeted = n - 1 + n_ell - 1
    if cut < m_size:
        pl.semaphore_signal(
            barrier, inc=1, device_id={"rad": across, "ell": lax.rem(my_ell + shift, n_ell)}, device_id_type=MESH
        )
        greeted += 1
    rows = pl.ds(pl.multiple_of(me * depth, depth), depth)
    fetches = [
        pltpu.make_async_copy(src, dst, fetch_sem.at[i])
        for i, (src, dst) in enumerate(((f_hbm, f_ref), (p_hbm, p_ref)))
    ]
    for copy in fetches:
        copy.start()

    def main(role):
        width = cut if role == 1 else m_size
        arrays = (
            (p_ref, stage_p, held_p, relay_p, n_size),
            (f_ref, stage_f, held_f, relay_f, width),
        )
        relayed = [(0, 0), (1, 0), (0, 1)] if role else []

        def stage(e):
            for src, staged, _, _, w in arrays:
                staged[e, :, :, :w] = jnp.swapaxes(src[:, e * n : (e + 1) * n, :w], 0, 1)

        def send(i, e, s):
            _, staged, held, _, w = arrays[i]
            peer = flipped(me, s, n)
            return pltpu.make_async_remote_copy(
                src_ref=staged.at[e, peer, :, pl.ds(0, w)],
                dst_ref=held.at[e, rows, pl.ds(0, w)],
                send_sem=send_sem.at[i, e, s],
                recv_sem=recv_sem.at[i, e, s],
                device_id={"rad": peer},
                device_id_type=MESH,
            )

        def to_relay(k):
            i, e = relayed[k]
            _, staged, _, relay, _ = arrays[i]
            return pltpu.make_async_remote_copy(
                src_ref=staged.at[e, across],
                dst_ref=relay.at[e],
                send_sem=send_sem.at[i, e, half],
                recv_sem=relay_sem.at[k],
                device_id={"ell": lax.rem(my_ell + shift, n_ell)},
                device_id_type=MESH,
            )

        def from_relay(k):
            i, e = relayed[k]
            _, _, held, relay, _ = arrays[i]
            return pltpu.make_async_remote_copy(
                src_ref=relay.at[e],
                dst_ref=held.at[e, rows],
                send_sem=relay_send.at[k],
                recv_sem=recv_sem.at[i, e, half],
                device_id={"rad": across, "ell": lax.rem(my_ell + shift, n_ell)},
                device_id_type=MESH,
            )

        locals_ = []
        arrivals = [[] for _ in range(own)]
        waits = []
        for copy in fetches:
            copy.wait()
        stage(0)
        pl.semaphore_wait(barrier, greeted)
        for e in range(own):
            for later in range(1 if e == 1 else e + 1, min(e + 2, own) if e else 0):
                stage(later)
            if role == 2:
                for k, (i, at) in enumerate(relayed):
                    if at == e:
                        copy = to_relay(k)
                        copy.start()
                        waits.append(copy)
                        arrivals[e].append(from_relay(k))
            for s in range(n - 1, 0, -1):
                for i in range(2):
                    if role == 2 and s == half and (i, e) in relayed:
                        continue
                    copy = send(i, e, s)
                    copy.start()
                    waits.append(copy)
                    arrivals[e].append(copy)
            for i, (_, staged, held, _, w) in enumerate(arrays):
                copy = pltpu.make_async_copy(
                    staged.at[e, me, :, pl.ds(0, w)], held.at[e, rows, pl.ds(0, w)], local_sem.at[i, e]
                )
                copy.start()
                locals_.append(copy)
            if role == 1 and e == 1:
                for k in range(len(relayed)):
                    to_relay(k).wait_recv()
                    copy = from_relay(k)
                    copy.start()
                    waits.append(copy)

        slots = lax.broadcasted_iota(jnp.int32, (width, n_size), 0)
        for e in range(own):
            locals_[2 * e].wait()
            locals_[2 * e + 1].wait()
            for copy in arrivals[e]:
                copy.wait_recv()
            coef = lax.dot_general(
                held_f[e, :, :width], held_p[e], (((0,), (0,)), ((), ())),
                preferred_element_type=jnp.float32,
            )
            valid = slots < 2 * ell_ref[e * n + me] + 1
            coef = jnp.where(valid, coef, 0.0)
            mine[e : e + 1, :] = jnp.sum(coef * coef, axis=0, keepdims=True)
            mine[own + e : own + e + 1, :] = jnp.max(jnp.abs(coef), axis=0, keepdims=True)

        copies = []
        for s in range(n - 1, 0, -1):
            copy = pltpu.make_async_remote_copy(
                src_ref=mine, dst_ref=stats.at[me], send_sem=send2.at[s], recv_sem=recv2.at[s],
                device_id={"rad": flipped(me, s, n)}, device_id_type=MESH,
            )
            copy.start()
            copies.append(copy)
        stats[me] = mine[...]
        for copy in copies:
            copy.wait_recv()
        every = stats[...]
        column = jnp.zeros((1, n_size), jnp.float32)
        top = jnp.zeros((1, n_size), jnp.float32)
        for s in range(n):
            column = column + jnp.sum(every[s, :own], axis=0, keepdims=True)
            top = jnp.maximum(top, jnp.max(every[s, own:], axis=0, keepdims=True))
        mine2[0:1, :] = column
        mine2[1:2, :] = top
        others = []
        for s in range(1, n_ell):
            copy = pltpu.make_async_remote_copy(
                src_ref=mine2, dst_ref=totals.at[my_ell], send_sem=send3.at[s], recv_sem=recv3.at[s],
                device_id={"ell": lax.rem(my_ell + s, n_ell)}, device_id_type=MESH,
            )
            copy.start()
            others.append(copy)
        totals[my_ell] = mine2[...]
        for copy in others:
            copy.wait_recv()
        both = totals[...]
        column = both[0, 0:1]
        top = both[0, 1:2]
        for s in range(1, n_ell):
            column = column + both[s, 0:1]
            top = jnp.maximum(top, both[s, 1:2])
        column = column + 1e-06
        top = top + 1e-06
        for e in range(own):
            for s in range(n):
                at = slice(e * n + s, e * n + s + 1)
                share_ref[at, :] = (n * own * n_ell) * every[s, e : e + 1] / column
                crest_ref[at, :] = every[s, own + e : own + e + 1] / top
        for copy in copies + others:
            copy.wait_send()
        for copy in waits:
            copy.wait_send()

    if cut < m_size:
        pl.when(my_ell < shift)(functools.partial(main, 1))
        pl.when(my_ell >= shift)(functools.partial(main, 2))
    else:
        main(0)


def by_ells(field, projection, ell_ids):
    n, n_ell = lax.axis_size("rad"), lax.axis_size("ell")
    depth, ells, m_size = field.shape
    n_size = projection.shape[2]
    own = ells // n
    most = m_size // 2 - 1 - (ells * n_ell - ells * (n_ell // 2))
    cut = min(m_size, -(-(2 * most + 1) // 128) * 128)
    if n_ell % 2 or own < 2 or cut < 128:
        cut = m_size
    vmem = pl.BlockSpec(memory_space=pltpu.VMEM)
    share, crest = pl.pallas_call(
        functools.partial(project_kernel, n, n_ell, own, depth, m_size, n_size, cut),
        out_shape=(
            jax.ShapeDtypeStruct((ells, n_size), jnp.float32),
            jax.ShapeDtypeStruct((ells, n_size), jnp.float32),
        ),
        in_specs=[pl.BlockSpec(memory_space=pltpu.SMEM)] + [pl.BlockSpec(memory_space=pl.ANY)] * 2,
        out_specs=(vmem, vmem),
        scratch_shapes=[
            pltpu.VMEM(field.shape, jnp.bfloat16),
            pltpu.VMEM(projection.shape, jnp.bfloat16),
            pltpu.SemaphoreType.DMA((2,)),
            pltpu.VMEM((own, n, depth, m_size), jnp.bfloat16),
            pltpu.VMEM((own, n, depth, n_size), jnp.bfloat16),
            pltpu.VMEM((own, n * depth, m_size), jnp.bfloat16),
            pltpu.VMEM((own, n * depth, n_size), jnp.bfloat16),
            pltpu.VMEM((2 * own, n_size), jnp.float32),
            pltpu.VMEM((n, 2 * own, n_size), jnp.float32),
            pltpu.VMEM((2, n_size), jnp.float32),
            pltpu.VMEM((n_ell, 2, n_size), jnp.float32),
            pltpu.VMEM((2, depth, m_size), jnp.bfloat16),
            pltpu.VMEM((2, depth, n_size), jnp.bfloat16),
            pltpu.SemaphoreType.DMA((2, own, n)),
            pltpu.SemaphoreType.DMA((2, own, n)),
            pltpu.SemaphoreType.DMA((2, own)),
            pltpu.SemaphoreType.DMA((3,)),
            pltpu.SemaphoreType.DMA((3,)),
            pltpu.SemaphoreType.DMA((n,)),
            pltpu.SemaphoreType.DMA((n,)),
            pltpu.SemaphoreType.DMA((n_ell,)),
            pltpu.SemaphoreType.DMA((n_ell,)),
        ],
        compiler_params=pltpu.CompilerParams(collective_id=0, has_side_effects=True),
    )(ell_ids, field, projection)
    width = n_size // n
    start = lax.axis_index("rad") * width
    return tuple(lax.dynamic_slice_in_dim(a, start, width, axis=1) for a in (share, crest))


def by_slots(field, projection, ell_ids):
    exchanged = lax.all_to_all(field, "rad", split_axis=2, concat_axis=0, tiled=True)
    slot_share = exchanged.shape[2]
    coef = jnp.einsum(
        "rem,ren->emn",
        exchanged,
        lax.all_gather(projection, "rad", axis=0, tiled=True),
        preferred_element_type=jnp.float32,
    )
    slots = lax.axis_index("rad") * slot_share + jnp.arange(slot_share, dtype=jnp.int32)
    valid = (slots[None, :] < 2 * ell_ids[:, None] + 1).astype(jnp.float32)
    energy_part = jnp.sum(valid[:, :, None] * coef * coef, axis=1)
    peak_part = jnp.max(valid[:, :, None] * jnp.abs(coef), axis=1)
    energy_all, peak_all = (
        lax.all_to_all(energy_part[None], "rad", split_axis=2, concat_axis=0, tiled=True),
        lax.all_to_all(peak_part[None], "rad", split_axis=2, concat_axis=0, tiled=True),
    )
    energy = jnp.sum(energy_all, axis=0)
    peak = jnp.max(peak_all, axis=0)
    column = lax.psum(jnp.sum(energy, axis=0), "ell") + 1e-06
    top = lax.pmax(jnp.max(peak, axis=0), "ell") + 1e-06
    total_ells = ell_ids.shape[0] * lax.axis_size("ell")
    share = total_ells * energy / column[None, :]
    crest = peak / top[None, :]
    return (share, crest)


def per_device(field, projection, ell_ids):
    n = lax.axis_size("rad")
    depth, ells, _ = field.shape
    if ells % n == 0 and n % 8 == 0 and n & (n - 1) == 0 and depth % 16 == 0:
        return by_ells(field, projection, ell_ids)
    return by_slots(field, projection, ell_ids)


def solution(mesh):
    in_specs = (P("rad", "ell", None), P("rad", "ell", None), P("ell"))
    out_specs = (P("ell", "rad"), P("ell", "rad"))
    return jax.shard_map(
        per_device, mesh=mesh, in_specs=in_specs, out_specs=out_specs, check_vma=False
    )
```

```python
import functools

import jax
import jax.numpy as jnp
from jax import lax
from jax.experimental import pallas as pl
from jax.experimental.pallas import tpu as pltpu
from jax.sharding import PartitionSpec as P

MESH = pl.DeviceIdType.MESH


def flipped(me, step, n):
    peer, bit = 0, 1
    while bit < n:
        b = (me // bit) % 2
        peer = peer + bit * ((1 - b) if step & bit else b)
        bit *= 2
    return peer


def project_kernel(n, n_ell, own, depth, m_size, n_size, cut, ell_ref, f_hbm, p_hbm, share_ref, crest_ref,
                   f_ref, p_ref, fetch_sem, stage_f, stage_p, held_f, held_p, mine, stats, mine2, totals,
                   relay_f, relay_p,
                   send_sem, recv_sem, local_sem, relay_sem, relay_send, send2, recv2, send3, recv3):
    me = lax.axis_index("rad")
    my_ell = lax.axis_index("ell")
    barrier = pltpu.get_barrier_semaphore()
    for s in range(1, n):
        pl.semaphore_signal(barrier, inc=1, device_id={"rad": flipped(me, s, n)}, device_id_type=MESH)
    for s in range(1, n_ell):
        pl.semaphore_signal(barrier, inc=1, device_id={"ell": lax.rem(my_ell + s, n_ell)}, device_id_type=MESH)

    shift, half = n_ell // 2, n // 2
    across = flipped(me, half, n)
    greeted = n - 1 + n_ell - 1
    if cut < m_size:
        pl.semaphore_signal(
            barrier, inc=1, device_id={"rad": across, "ell": lax.rem(my_ell + shift, n_ell)}, device_id_type=MESH
        )
        greeted += 1
    rows = pl.ds(pl.multiple_of(me * depth, depth), depth)
    fetches = [
        pltpu.make_async_copy(src, dst, fetch_sem.at[i])
        for i, (src, dst) in enumerate(((f_hbm, f_ref), (p_hbm, p_ref)))
    ]
    for copy in fetches:
        copy.start()

    def main(role):
        width = cut if role == 1 else m_size
        arrays = (
            (p_ref, stage_p, held_p, relay_p, n_size),
            (f_ref, stage_f, held_f, relay_f, width),
        )
        relayed = [(0, 0), (1, 0), (0, 1)] if role else []

        def stage(e):
            for src, staged, _, _, w in arrays:
                staged[e, :, :, :w] = jnp.swapaxes(src[:, e * n : (e + 1) * n, :w], 0, 1)

        def send(i, e, s):
            _, staged, held, _, w = arrays[i]
            peer = flipped(me, s, n)
            return pltpu.make_async_remote_copy(
                src_ref=staged.at[e, peer, :, pl.ds(0, w)],
                dst_ref=held.at[e, rows, pl.ds(0, w)],
                send_sem=send_sem.at[i, e, s],
                recv_sem=recv_sem.at[i, e, s],
                device_id={"rad": peer},
                device_id_type=MESH,
            )

        def to_relay(k):
            i, e = relayed[k]
            _, staged, _, relay, _ = arrays[i]
            return pltpu.make_async_remote_copy(
                src_ref=staged.at[e, across],
                dst_ref=relay.at[e],
                send_sem=send_sem.at[i, e, half],
                recv_sem=relay_sem.at[k],
                device_id={"ell": lax.rem(my_ell + shift, n_ell)},
                device_id_type=MESH,
            )

        def from_relay(k):
            i, e = relayed[k]
            _, _, held, relay, _ = arrays[i]
            return pltpu.make_async_remote_copy(
                src_ref=relay.at[e],
                dst_ref=held.at[e, rows],
                send_sem=relay_send.at[k],
                recv_sem=recv_sem.at[i, e, half],
                device_id={"rad": across, "ell": lax.rem(my_ell + shift, n_ell)},
                device_id_type=MESH,
            )

        locals_ = []
        arrivals = [[] for _ in range(own)]
        waits = []
        for copy in fetches:
            copy.wait()
        stage(0)
        pl.semaphore_wait(barrier, greeted)
        for e in range(own):
            for later in range(1 if e == 1 else e + 1, min(e + 2, own) if e else 0):
                stage(later)
            if role == 2:
                for k, (i, at) in enumerate(relayed):
                    if at == e:
                        copy = to_relay(k)
                        copy.start()
                        waits.append(copy)
                        arrivals[e].append(from_relay(k))
            for s in [*range(half - 1, 0, -1), *range(n - 1, half - 1, -1)]:
                for i in range(2):
                    if role == 2 and s == half and (i, e) in relayed:
                        continue
                    copy = send(i, e, s)
                    copy.start()
                    waits.append(copy)
                    arrivals[e].append(copy)
            for i, (_, staged, held, _, w) in enumerate(arrays):
                copy = pltpu.make_async_copy(
                    staged.at[e, me, :, pl.ds(0, w)], held.at[e, rows, pl.ds(0, w)], local_sem.at[i, e]
                )
                copy.start()
                locals_.append(copy)
            if role == 1 and e == 1:
                for k in range(len(relayed)):
                    to_relay(k).wait_recv()
                    copy = from_relay(k)
                    copy.start()
                    waits.append(copy)

        slots = lax.broadcasted_iota(jnp.int32, (width, n_size), 0)
        for e in range(own):
            locals_[2 * e].wait()
            locals_[2 * e + 1].wait()
            for copy in arrivals[e]:
                copy.wait_recv()
            coef = lax.dot_general(
                held_f[e, :, :width], held_p[e], (((0,), (0,)), ((), ())),
                preferred_element_type=jnp.float32,
            )
            valid = slots < 2 * ell_ref[e * n + me] + 1
            coef = jnp.where(valid, coef, 0.0)
            mine[e : e + 1, :] = jnp.sum(coef * coef, axis=0, keepdims=True)
            mine[own + e : own + e + 1, :] = jnp.max(jnp.abs(coef), axis=0, keepdims=True)

        copies = []
        for s in range(n - 1, 0, -1):
            copy = pltpu.make_async_remote_copy(
                src_ref=mine, dst_ref=stats.at[me], send_sem=send2.at[s], recv_sem=recv2.at[s],
                device_id={"rad": flipped(me, s, n)}, device_id_type=MESH,
            )
            copy.start()
            copies.append(copy)
        stats[me] = mine[...]
        for copy in copies:
            copy.wait_recv()
        every = stats[...]
        column = jnp.zeros((1, n_size), jnp.float32)
        top = jnp.zeros((1, n_size), jnp.float32)
        for s in range(n):
            column = column + jnp.sum(every[s, :own], axis=0, keepdims=True)
            top = jnp.maximum(top, jnp.max(every[s, own:], axis=0, keepdims=True))
        mine2[0:1, :] = column
        mine2[1:2, :] = top
        others = []
        for s in range(1, n_ell):
            copy = pltpu.make_async_remote_copy(
                src_ref=mine2, dst_ref=totals.at[my_ell], send_sem=send3.at[s], recv_sem=recv3.at[s],
                device_id={"ell": lax.rem(my_ell + s, n_ell)}, device_id_type=MESH,
            )
            copy.start()
            others.append(copy)
        totals[my_ell] = mine2[...]
        for copy in others:
            copy.wait_recv()
        both = totals[...]
        column = both[0, 0:1]
        top = both[0, 1:2]
        for s in range(1, n_ell):
            column = column + both[s, 0:1]
            top = jnp.maximum(top, both[s, 1:2])
        column = column + 1e-06
        top = top + 1e-06
        for e in range(own):
            for s in range(n):
                at = slice(e * n + s, e * n + s + 1)
                share_ref[at, :] = (n * own * n_ell) * every[s, e : e + 1] / column
                crest_ref[at, :] = every[s, own + e : own + e + 1] / top
        for copy in copies + others:
            copy.wait_send()
        for copy in waits:
            copy.wait_send()

    if cut < m_size:
        pl.when(my_ell < shift)(functools.partial(main, 1))
        pl.when(my_ell >= shift)(functools.partial(main, 2))
    else:
        main(0)


def by_ells(field, projection, ell_ids):
    n, n_ell = lax.axis_size("rad"), lax.axis_size("ell")
    depth, ells, m_size = field.shape
    n_size = projection.shape[2]
    own = ells // n
    most = m_size // 2 - 1 - (ells * n_ell - ells * (n_ell // 2))
    cut = min(m_size, -(-(2 * most + 1) // 128) * 128)
    if n_ell % 2 or own < 2 or cut < 128:
        cut = m_size
    vmem = pl.BlockSpec(memory_space=pltpu.VMEM)
    share, crest = pl.pallas_call(
        functools.partial(project_kernel, n, n_ell, own, depth, m_size, n_size, cut),
        out_shape=(
            jax.ShapeDtypeStruct((ells, n_size), jnp.float32),
            jax.ShapeDtypeStruct((ells, n_size), jnp.float32),
        ),
        in_specs=[pl.BlockSpec(memory_space=pltpu.SMEM)] + [pl.BlockSpec(memory_space=pl.ANY)] * 2,
        out_specs=(vmem, vmem),
        scratch_shapes=[
            pltpu.VMEM(field.shape, jnp.bfloat16),
            pltpu.VMEM(projection.shape, jnp.bfloat16),
            pltpu.SemaphoreType.DMA((2,)),
            pltpu.VMEM((own, n, depth, m_size), jnp.bfloat16),
            pltpu.VMEM((own, n, depth, n_size), jnp.bfloat16),
            pltpu.VMEM((own, n * depth, m_size), jnp.bfloat16),
            pltpu.VMEM((own, n * depth, n_size), jnp.bfloat16),
            pltpu.VMEM((2 * own, n_size), jnp.float32),
            pltpu.VMEM((n, 2 * own, n_size), jnp.float32),
            pltpu.VMEM((2, n_size), jnp.float32),
            pltpu.VMEM((n_ell, 2, n_size), jnp.float32),
            pltpu.VMEM((2, depth, m_size), jnp.bfloat16),
            pltpu.VMEM((2, depth, n_size), jnp.bfloat16),
            pltpu.SemaphoreType.DMA((2, own, n)),
            pltpu.SemaphoreType.DMA((2, own, n)),
            pltpu.SemaphoreType.DMA((2, own)),
            pltpu.SemaphoreType.DMA((3,)),
            pltpu.SemaphoreType.DMA((3,)),
            pltpu.SemaphoreType.DMA((n,)),
            pltpu.SemaphoreType.DMA((n,)),
            pltpu.SemaphoreType.DMA((n_ell,)),
            pltpu.SemaphoreType.DMA((n_ell,)),
        ],
        compiler_params=pltpu.CompilerParams(collective_id=0, has_side_effects=True),
    )(ell_ids, field, projection)
    width = n_size // n
    start = lax.axis_index("rad") * width
    return tuple(lax.dynamic_slice_in_dim(a, start, width, axis=1) for a in (share, crest))


def by_slots(field, projection, ell_ids):
    exchanged = lax.all_to_all(field, "rad", split_axis=2, concat_axis=0, tiled=True)
    slot_share = exchanged.shape[2]
    coef = jnp.einsum(
        "rem,ren->emn",
        exchanged,
        lax.all_gather(projection, "rad", axis=0, tiled=True),
        preferred_element_type=jnp.float32,
    )
    slots = lax.axis_index("rad") * slot_share + jnp.arange(slot_share, dtype=jnp.int32)
    valid = (slots[None, :] < 2 * ell_ids[:, None] + 1).astype(jnp.float32)
    energy_part = jnp.sum(valid[:, :, None] * coef * coef, axis=1)
    peak_part = jnp.max(valid[:, :, None] * jnp.abs(coef), axis=1)
    energy_all, peak_all = (
        lax.all_to_all(energy_part[None], "rad", split_axis=2, concat_axis=0, tiled=True),
        lax.all_to_all(peak_part[None], "rad", split_axis=2, concat_axis=0, tiled=True),
    )
    energy = jnp.sum(energy_all, axis=0)
    peak = jnp.max(peak_all, axis=0)
    column = lax.psum(jnp.sum(energy, axis=0), "ell") + 1e-06
    top = lax.pmax(jnp.max(peak, axis=0), "ell") + 1e-06
    total_ells = ell_ids.shape[0] * lax.axis_size("ell")
    share = total_ells * energy / column[None, :]
    crest = peak / top[None, :]
    return (share, crest)


def per_device(field, projection, ell_ids):
    n = lax.axis_size("rad")
    depth, ells, _ = field.shape
    if ells % n == 0 and n % 8 == 0 and n & (n - 1) == 0 and depth % 16 == 0:
        return by_ells(field, projection, ell_ids)
    return by_slots(field, projection, ell_ids)


def solution(mesh):
    in_specs = (P("rad", "ell", None), P("rad", "ell", None), P("ell"))
    out_specs = (P("ell", "rad"), P("ell", "rad"))
    return jax.shard_map(
        per_device, mesh=mesh, in_specs=in_specs, out_specs=out_specs, check_vma=False
    )
```
